32 devices in a mesh: rec: 4 (over y, x), win: 8 (over z, core).
Axes of the slice: x: 2, y: 2, z: 4, core: 2. Of those that a mesh axis runs over, the one named last changes fastest.
Arguments:
- strain: bfloat16 [1024, 32, 2176], P('rec', 'win'), may hold values from -90 to 90
- sources: int32 [256], replicated, may hold values from 0 to 1023, as said below
- offsets: int32 [32], P('win'), may hold values from 0 to 128
Outputs:
- cross: bfloat16 [2, 256, 512, 1024], P(None, None, 'win', 'rec')
The draws below stay inside these ranges and needn't reach their ends.
Inputs may be any that keep to these rules, and one draw needn't show every extreme that they name: sources are distinct; among the channels i * 256 to (i + 1) * 256 - 1 of any i there are at most 128 of them, and exactly 128 for some i.
All inputs are finite; a program needn't handle non-finite values.
Results may differ from the reference program's by a relative error of at most 0.0057.
Values may be sent and summed in bfloat16 or wider, within the bound.
No kernel may reach another device: no remote copies, remote signals or barrier semaphores. Data moves between devices by JAX's collectives and lax.ppermute only.
A program may use at most 128 MiB of HBM per device.

```python
import math
import jax
import jax.numpy as jnp
from jax import lax

NT = 2048
NF = 512
F_LO = 10
SUB = 64
SLACK = 128
NS = 256
C_DEV = 256
SEG = 2176
CHANNELS = 1024
RECORDS = 32
SRC_MOST = 128


def draw_strain(key, part):
    key_noise, key_tilt, key_amp = jax.random.split(key, 3)
    shape = (CHANNELS, RECORDS, SEG)
    noise = jnp.clip(jax.random.normal(key_noise, shape, jnp.float32), -5.0, 5.0)
    top = math.log(10.0)
    tilt = jax.random.uniform(key_tilt, (CHANNELS, 1, 1), jnp.float32, -0.8, 0.8)
    coloured = noise + tilt * jnp.roll(noise, 1, axis=2)
    amplitude = jnp.exp(jax.random.uniform(key_amp, (CHANNELS, RECORDS, 1), jnp.float32, 0.0, top))
    return (coloured * amplitude).astype(jnp.bfloat16)


def draw_sources(key, part):
    owners_total = CHANNELS // C_DEV
    most = SRC_MOST
    key_heavy, key_slots, key_tables, key_order = jax.random.split(jax.random.fold_in(key, 7), 4)
    heavy = jax.random.randint(key_heavy, (), 0, owners_total, dtype=jnp.int32)
    spread = jax.random.permutation(key_slots, jnp.arange((owners_total - 1) * most, dtype=jnp.int32))[:NS - most]
    other_owner = (heavy + 1 + spread // most) % owners_total
    owner = jnp.concatenate((jnp.full((most,), heavy, jnp.int32), other_owner.astype(jnp.int32)))
    slot = jnp.concatenate((jnp.arange(most, dtype=jnp.int32), (spread % most).astype(jnp.int32)))
    tables = jax.vmap(lambda table_key: jax.random.permutation(table_key, jnp.arange(C_DEV, dtype=jnp.int32)))(jax.random.split(key_tables, owners_total))
    channel = owner * C_DEV + tables[owner, slot]
    return jax.random.permutation(key_order, channel).astype(jnp.int32)


def plant(array, own_key, least, high):
    shape = array.shape
    index_at = [jax.random.randint(jax.random.fold_in(own_key, axis), (), 0, shape[axis]) for axis in range(len(shape))]
    array = array.at[tuple(index_at)].set(least)
    longest = shape.index(max(shape))
    index_at[longest] = (index_at[longest] + 1) % shape[longest]
    return array.at[tuple(index_at)].set(high)


def setup_inputs(seed: int = 0) -> dict:
    key_list = jax.random.split(jax.random.key(seed), 4)
    return {
        "strain": draw_strain(jax.random.fold_in(key_list[3], 71), 0),
        "sources": draw_sources(jax.random.fold_in(key_list[3], 71), 0),
        "offsets": plant(jax.random.randint(key_list[2], (RECORDS,), 0, SLACK + 1), jax.random.fold_in(key_list[2], 1), 0, SLACK).astype(jnp.int32),
    }


EPSILON = 1e-06

def taper_window(length):
    edge = length // 16
    sample = jnp.arange(length, dtype=jnp.float32)
    rising = 0.5 * (1.0 - jnp.cos(math.pi * (sample + 0.5) / edge))
    falling = 0.5 * (1.0 - jnp.cos(math.pi * (length - sample - 0.5) / edge))
    return jnp.where(sample < edge, rising, jnp.where(sample >= length - edge, falling, 1.0))

def whiten(spectra):
    dims = spectra.shape
    blocks = spectra.reshape(dims[0], dims[1] // SUB, SUB, dims[2], dims[3])
    power = lax.optimization_barrier(jnp.mean(blocks[0] * blocks[0] + blocks[1] * blocks[1], axis=1, keepdims=True))
    return (blocks * lax.rsqrt(power + EPSILON)).reshape(dims).astype(jnp.bfloat16)

def reference(strain, sources, offsets):
    taper = taper_window(NT)

    def one_record(number):
        trace = lax.dynamic_slice_in_dim(strain, number, 1, 1)[:, 0, :]
        begin_at = lax.dynamic_index_in_dim(offsets, number, keepdims=False)
        piece = lax.dynamic_slice_in_dim(trace, begin_at.astype(jnp.int32), NT, 1).astype(jnp.float32)
        centred = piece - lax.optimization_barrier(jnp.mean(piece, axis=-1, keepdims=True))
        tapered = centred * taper
        spectrum = jnp.fft.rfft(tapered, axis=-1)[:, F_LO:F_LO + NF]
        stacked = jnp.stack((jnp.real(spectrum), jnp.imag(spectrum)))
        return whiten(jnp.transpose(stacked, (0, 2, 1))[:, :, None, :])[:, :, 0, :]
    white = lax.map(one_record, jnp.arange(RECORDS, dtype=jnp.int32))
    by_bin = jnp.transpose(white, (2, 0, 1, 3))

    def one_bin(block):
        whole = block.astype(jnp.float32)
        source_spec = whole[:, :, sources]
        turned = jnp.stack((source_spec[:, 1], -source_spec[:, 0]), axis=1)
        real_part = jnp.einsum('rqs,rqc->sc', source_spec, whole)
        imag_part = jnp.einsum('rqs,rqc->sc', turned, whole)
        return (jnp.stack((real_part, imag_part)) / RECORDS).astype(jnp.bfloat16)
    crossed = lax.map(one_bin, by_bin)
    return jnp.transpose(crossed, (1, 2, 0, 3))
```

```python
import functools
import math

import jax
import jax.numpy as jnp
import numpy as np
from jax import lax
from jax.experimental import pallas as pl
from jax.experimental.pallas import tpu as pltpu
from jax.sharding import PartitionSpec as P

NT = 2048
NF = 512
F_LO = 10
SUB = 64
HALF = NT // 2
LANES = 128
NBAND = NF // SUB
PAIRS = SUB // 2
CHUNKS = 2
JBLOCK = 16

EPSILON = 1e-06

NT_DIMS = (((1,), (1,)), ((), ()))


def table_parts():
    pair = np.arange(PAIRS)
    band = np.arange(NBAND)
    beta_sample = np.arange(LANES)
    fine = np.zeros((2, 2, NBAND, PAIRS, LANES), np.float64)
    coarse = np.zeros((2, 2, 2, 8, HALF), np.float64)
    row = np.arange(8)
    step = np.arange(HALF) // LANES
    for parity in range(2):
        bins = F_LO + band[:, None] * SUB + 2 * pair[None, :] + parity
        beta = 2.0 * np.pi * (bins[..., None] * beta_sample % NT) / NT
        fine[0, parity], fine[1, parity] = np.cos(beta), np.sin(beta)
        turns = (F_LO + 2 * row + parity)[:, None] * step[None, :] % 16
        for part in range(2):
            alpha = 2.0 * np.pi * turns / 16.0 + part * np.pi / 2.0
            coarse[0, parity, part], coarse[1, parity, part] = np.cos(alpha), np.sin(alpha)
    return fine.astype(np.float32), coarse.astype(np.float32)


def front_kernel(rows_dev, wins, offs, strain, perm, fine, coarse, *rest):
    outs = rest[: 2 * CHUNKS]
    high, low, table_high, table_low, spec, laid = rest[2 * CHUNKS :]
    chan, _, seg = strain.shape
    bins_dev = NF // wins

    for parity in range(2):
        for part in range(2):
            for step in range(HALF // LANES):
                at = pl.ds(step * LANES, LANES)
                cos_a = coarse[0, parity, part, :, at]
                sin_a = coarse[1, parity, part, :, at]
                cos_b = fine[0, parity].reshape(NBAND * PAIRS // 8, 8, LANES)
                sin_b = fine[1, parity].reshape(NBAND * PAIRS // 8, 8, LANES)
                value = (cos_a[None] * cos_b - sin_a[None] * sin_b).reshape(NBAND, PAIRS, LANES)
                top = value.astype(jnp.bfloat16)
                table_high[parity, :, pl.ds(part * PAIRS, PAIRS), at] = top
                table_low[parity, :, pl.ds(part * PAIRS, PAIRS), at] = (
                    value - top.astype(jnp.float32)
                ).astype(jnp.bfloat16)

    edge = NT // 16
    place = lax.broadcasted_iota(jnp.int32, (8, seg), 1)
    number = lax.broadcasted_iota(jnp.int32, (8, seg), 0)
    begin = jnp.zeros((8, seg), jnp.int32)
    for r in range(rows_dev):
        begin = jnp.where(number == r, offs[r], begin)
    sample = place - begin
    inside = (sample >= 0) & (sample < NT)
    near = jnp.minimum(sample, NT - 1 - sample).astype(jnp.float32) + 0.5
    slope = 0.5 * (1.0 - jnp.cos(near * (math.pi / edge)))
    taper = jnp.where(inside, jnp.where(near < edge, slope, 1.0), 0.0)
    window = jnp.where(inside, 1.0, 0.0)

    step_rows = 16

    def prepare(i, carry):
        at = pl.ds(pl.multiple_of(i * step_rows, step_rows), step_rows)
        for r in range(rows_dev):
            x = strain[at, r, :].astype(jnp.float32)
            mean = jnp.sum(x * window[r : r + 1], axis=1, keepdims=True) * (1.0 / NT)
            z = (x - mean) * taper[r : r + 1]
            first = jnp.concatenate((z[:, : seg - NT] + z[:, NT:], z[:, seg - NT : HALF]), axis=1)
            second = z[:, HALF:NT]
            for parity, folded in enumerate((first + second, first - second)):
                top = folded.astype(jnp.bfloat16)
                high[r, parity, at, :] = top
                low[r, parity, at, :] = (folded - top.astype(jnp.float32)).astype(jnp.bfloat16)
        return carry

    lax.fori_loop(0, chan // step_rows, prepare, 0)

    rows = NBAND * SUB
    for r in range(rows_dev):
        for parity in range(2):
            t_high = table_high[parity].reshape(rows, HALF)
            t_low = table_low[parity].reshape(rows, HALF)
            x_high, x_low = high[r, parity], low[r, parity]
            dot = functools.partial(
                lax.dot_general, dimension_numbers=NT_DIMS, preferred_element_type=jnp.float32
            )
            spec[parity] = dot(t_high, x_high) + dot(t_high, x_low) + dot(t_low, x_high)

        off = offs[r]
        pair = lax.broadcasted_iota(jnp.int32, (PAIRS, LANES), 0)
        turn = 2.0 * math.pi / NT
        inner = []
        for parity in range(2):
            angle = (((F_LO + 2 * pair + parity) * off) & (NT - 1)).astype(jnp.float32) * turn
            inner.append((jnp.cos(angle), jnp.sin(angle)))
        band_no = lax.broadcasted_iota(jnp.int32, (NBAND, LANES), 0)
        angle = ((SUB * band_no * off) & (NT - 1)).astype(jnp.float32) * turn
        band_cos, band_sin = jnp.cos(angle), jnp.sin(angle)

        for band in range(NBAND):
            total = None
            for parity in range(2):
                block = spec[parity, pl.ds(band * SUB, SUB), :]
                energy = jnp.sum(block * block, axis=0, keepdims=True)
                total = energy if total is None else total + energy
            scale = lax.rsqrt(total * (1.0 / SUB) + EPSILON)
            bc, bs = band_cos[band : band + 1], band_sin[band : band + 1]
            for parity in range(2):
                ic, is_ = inner[parity]
                cos = ic * bc - is_ * bs
                sin = ic * bs + is_ * bc
                for lane in range(chan // LANES):
                    lanes = pl.ds(lane * LANES, LANES)
                    scale_l = scale[:, lane * LANES : (lane + 1) * LANES]
                    real = spec[parity, pl.ds(band * SUB, PAIRS), lanes] * scale_l
                    imag = spec[parity, pl.ds(band * SUB + PAIRS, PAIRS), lanes] * scale_l
                    for part, value in enumerate((real * cos - imag * sin, real * sin + imag * cos)):
                        start = band * SUB * 2 * rows_dev + parity * 2 * rows_dev + part * rows_dev + r
                        laid[lane, pl.ds(start, PAIRS, stride=4 * rows_dev), :] = value

    per_win = bins_dev * 2 * rows_dev
    per_chunk = per_win // CHUNKS

    def emit(w, carry):
        at = pl.ds(pl.multiple_of(w * per_win, per_win), per_win)
        white = jnp.concatenate(
            [laid[lane, at, :].astype(jnp.bfloat16) for lane in range(chan // LANES)], axis=1
        )
        placed = jnp.dot(white, perm[...], preferred_element_type=jnp.float32).astype(jnp.bfloat16)
        for k in range(CHUNKS):
            piece = placed[k * per_chunk : (k + 1) * per_chunk]
            for half in range(2):
                outs[2 * k + half][w] = piece[:, half * LANES : (half + 1) * LANES]
        return carry

    lax.fori_loop(0, wins, emit, 0)


def front(strain, offsets, perm, wins):
    chan, rows_dev, seg = strain.shape
    rows = NF // wins * 2 * rows_dev // CHUNKS
    fine, coarse = table_parts()
    vmem = pl.BlockSpec(memory_space=pltpu.VMEM)
    return pl.pallas_call(
        functools.partial(front_kernel, rows_dev, wins),
        out_shape=[jax.ShapeDtypeStruct((wins, rows, LANES), jnp.bfloat16)] * (2 * CHUNKS),
        in_specs=[pl.BlockSpec(memory_space=pltpu.SMEM)] + [vmem] * 4,
        out_specs=[vmem] * (2 * CHUNKS),
        scratch_shapes=[
            pltpu.VMEM((rows_dev, 2, chan, HALF), jnp.bfloat16),
            pltpu.VMEM((rows_dev, 2, chan, HALF), jnp.bfloat16),
            pltpu.VMEM((2, NBAND, SUB, HALF), jnp.bfloat16),
            pltpu.VMEM((2, NBAND, SUB, HALF), jnp.bfloat16),
            pltpu.VMEM((2, NBAND * SUB, chan), jnp.float32),
            pltpu.VMEM((chan // LANES, NF * 2 * rows_dev, LANES), jnp.float32),
        ],
        compiler_params=pltpu.CompilerParams(vmem_limit_bytes=56 * 2**20),
        name="front",
    )(offsets, strain, perm, jnp.asarray(fine), jnp.asarray(coarse))


def cross_kernel(rows_dev, wins, records, *refs):
    owners_refs, (other, perm, select), out, laid = refs[:-5], refs[-5:-2], refs[-2], refs[-1]
    mine = owners_refs[0]
    columns = select.shape[1] // LANES
    owners_refs = owners_refs[-columns:]
    depth = 2 * rows_dev * wins
    group = 256 // depth
    near = 2 * rows_dev * group
    width = wins * near
    sources = select.shape[0]
    scale = 1.0 / records

    lane = lax.broadcasted_iota(jnp.int32, (1, width), 1)
    row_no = lax.broadcasted_iota(jnp.int32, (width, width), 0)
    col_no = lax.broadcasted_iota(jnp.int32, (width, width), 1)
    first = (col_no // rows_dev) % 2 == 0
    turn = jnp.where(
        first & (row_no == col_no + rows_dev),
        1.0,
        jnp.where(jnp.logical_not(first) & (row_no == col_no - rows_dev), -1.0, 0.0),
    ).astype(jnp.bfloat16)
    keep = [((lane // (2 * rows_dev)) % group == b).astype(jnp.bfloat16) for b in range(group)]

    for g in range(JBLOCK // group):
        at = pl.ds(g * near, near)

        def rows_of(ref):
            return ref[:, at, :].reshape(width, LANES)

        slots = jnp.concatenate((rows_of(mine), rows_of(other)), axis=1)
        receivers = lax.dot_general(
            slots, perm[...], NT_DIMS, preferred_element_type=jnp.float32
        ).astype(jnp.bfloat16)
        held = jnp.concatenate([rows_of(ref) for ref in owners_refs], axis=1)
        picked = lax.dot_general(
            select[...], held, NT_DIMS, preferred_element_type=jnp.float32
        ).astype(jnp.bfloat16)
        turned = jnp.dot(picked, turn, preferred_element_type=jnp.float32).astype(jnp.bfloat16)
        for b in range(group):
            both = jnp.concatenate((picked * keep[b], turned * keep[b]), axis=0)
            product = jnp.dot(both, receivers, preferred_element_type=jnp.float32)
            for part in range(2):
                for half in range(product.shape[1] // LANES):
                    laid[part, half, pl.ds(g * group + b, sources, stride=JBLOCK), :] = product[
                        part * sources : (part + 1) * sources, half * LANES : (half + 1) * LANES
                    ]

    few = 16

    def emit(i, carry):
        rows = pl.ds(pl.multiple_of(i * few * JBLOCK, few * JBLOCK), few * JBLOCK)
        at = pl.ds(pl.multiple_of(i * few, few), few)
        for part in range(2):
            for half in range(laid.shape[1]):
                value = (laid[part, half, rows, :] * scale).astype(jnp.bfloat16)
                out[part, at, :, half * LANES : (half + 1) * LANES] = value.reshape(few, JBLOCK, LANES)
        return carry

    lax.fori_loop(0, sources // few, emit, 0)


def cross(k, whole, owners, other, perm, select, shape, records, rows_dev):
    wins, rows, _ = other.shape
    sources, chan = shape[1], shape[3]
    per_block = JBLOCK * 2 * rows_dev
    steps = rows // per_block
    piece = pl.BlockSpec((wins, per_block, LANES), lambda g: (0, g, 0))
    fixed = lambda array: pl.BlockSpec(array.shape, lambda g: (0, 0))
    args = list(owners) + [other, perm, select]
    specs = [piece] * (len(owners) + 1) + [fixed(perm), fixed(select)]
    body = functools.partial(cross_kernel, rows_dev, wins, records)
    aliases = {}
    if whole is not None:
        inner, count = body, len(args)
        body = lambda *refs: inner(*refs[:count], *refs[count + 1 :])
        aliases = {count: 0}
        args.append(whole)
        specs.append(pl.BlockSpec(memory_space=pl.ANY))
    return pl.pallas_call(
        body,
        grid=(steps,),
        out_shape=jax.ShapeDtypeStruct(shape, jnp.bfloat16),
        in_specs=specs,
        out_specs=pl.BlockSpec((2, sources, JBLOCK, chan), lambda g: (0, 0, k * steps + g, 0)),
        scratch_shapes=[pltpu.VMEM((2, chan // LANES, sources * JBLOCK, LANES), jnp.float32)],
        input_output_aliases=aliases,
        compiler_params=pltpu.CompilerParams(vmem_limit_bytes=56 * 2**20),
        name=f"cross{k}",
    )(*args)


def body(recs, wins, strain, sources, offsets):
    chan, rows_dev, _ = strain.shape
    me = lax.axis_index("rec")
    channel = jnp.arange(chan, dtype=jnp.int32)
    local = sources - me * chan
    hit = jnp.any(local[None, :] == channel[:, None], axis=1).astype(jnp.int32)
    ahead = jnp.sum(jnp.where(channel[None, :] < channel[:, None], hit[None, :], 0), axis=1)
    slot = jnp.where(hit > 0, ahead, jnp.sum(hit) + channel - ahead)
    perm = (slot[:, None] == channel[None, :]).astype(jnp.bfloat16)
    owner = sources // chan
    rank = jnp.sum(
        (owner[None, :] == owner[:, None]) & (sources[None, :] < sources[:, None]), axis=1
    ).astype(jnp.int32)
    if recs == 4:
        order = me ^ jnp.arange(4, dtype=jnp.int32)
    else:
        order = jnp.arange(recs, dtype=jnp.int32)
    place = jnp.arange(LANES, dtype=jnp.int32)
    select = (
        (owner[:, None, None] == order[None, :, None]) & (rank[:, None, None] == place[None, None, :])
    ).astype(jnp.bfloat16).reshape(sources.shape[0], recs * LANES)

    pieces = front(strain, offsets, perm, wins)

    def swap(array, bit):
        return lax.ppermute(array, "rec", [(i, i ^ bit) for i in range(recs)])

    def spread(array):
        return lax.all_to_all(array, "win", split_axis=0, concat_axis=0, tiled=True)

    owners = []
    for k in range(CHUNKS):
        mine = spread(pieces[2 * k])
        if recs == 4:
            along_x, along_y = swap(mine, 1), swap(mine, 2)
            far = swap(along_x, 2) if k % 2 == 0 else swap(along_y, 1)
            owners.append((mine, along_x, along_y, far))
        else:
            gathered = lax.all_gather(mine, "rec", axis=0)
            owners.append((mine,) + tuple(gathered[i] for i in range(recs)))
    shape = (2, sources.shape[0], NF // wins, chan)
    whole = None
    for k in range(CHUNKS):
        other = spread(pieces[2 * k + 1])
        whole = cross(k, whole, owners[k], other, perm, select, shape, rows_dev * wins, rows_dev)
    return whole


def solution(mesh):
    recs, wins = mesh.shape["rec"], mesh.shape["win"]
    placed = (P("rec", "win", None), P(), P("win"))
    return jax.shard_map(
        functools.partial(body, recs, wins),
        mesh=mesh,
        in_specs=placed,
        out_specs=P(None, None, "win", "rec"),
        check_vma=False,
    )
```

```python
import functools
import math

import jax
import jax.numpy as jnp
import numpy as np
from jax import lax
from jax.experimental import pallas as pl
from jax.experimental.pallas import tpu as pltpu
from jax.sharding import PartitionSpec as P

NT = 2048
NF = 512
F_LO = 10
SUB = 64
HALF = NT // 2
LANES = 128
NBAND = NF // SUB
PAIRS = SUB // 2
CHUNKS = 2
JBLOCK = 16
PITCH = JBLOCK + 4

EPSILON = 1e-06

NT_DIMS = (((1,), (1,)), ((), ()))


def table_parts():
    pair = np.arange(PAIRS)
    band = np.arange(NBAND)
    beta_sample = np.arange(LANES)
    fine = np.zeros((2, 2, NBAND, PAIRS, LANES), np.float64)
    coarse = np.zeros((2, 2, 2, 8, HALF), np.float64)
    row = np.arange(8)
    step = np.arange(HALF) // LANES
    for parity in range(2):
        bins = F_LO + band[:, None] * SUB + 2 * pair[None, :] + parity
        beta = 2.0 * np.pi * (bins[..., None] * beta_sample % NT) / NT
        fine[0, parity], fine[1, parity] = np.cos(beta), np.sin(beta)
        turns = (F_LO + 2 * row + parity)[:, None] * step[None, :] % 16
        for part in range(2):
            alpha = 2.0 * np.pi * turns / 16.0 + part * np.pi / 2.0
            coarse[0, parity, part], coarse[1, parity, part] = np.cos(alpha), np.sin(alpha)
    return fine.astype(np.float32), coarse.astype(np.float32)


def front_kernel(rows_dev, wins, offs, mesh_row, sources, strain_hbm, fine, coarse, *rest):
    pieces, perm = rest[: 1 + CHUNKS], rest[1 + CHUNKS]
    strain, high, low, table_high, table_low, spec, laid, fold, arrived = rest[2 + CHUNKS :]
    chan, _, seg = strain.shape
    bins_dev = NF // wins
    fetch = pltpu.make_async_copy(strain_hbm, strain, arrived)
    fetch.start()

    count = sources.shape[1]
    own = sources[...] - mesh_row[0] * chan
    channel = lax.broadcasted_iota(jnp.int32, (chan, count), 0)
    match = jnp.where(own == channel, 1.0, 0.0)
    hit = jnp.sum(match, axis=1, keepdims=True)
    before = lax.broadcasted_iota(jnp.int32, (chan, chan), 1)
    after = lax.broadcasted_iota(jnp.int32, (chan, chan), 0)
    earlier = jnp.where(before < after, 1.0, 0.0).astype(jnp.bfloat16)
    ahead = jnp.sum(
        jnp.dot(earlier, match.astype(jnp.bfloat16), preferred_element_type=jnp.float32),
        axis=1,
        keepdims=True,
    )
    here = after[:, :1].astype(jnp.float32)
    slot = jnp.where(hit > 0.0, ahead, jnp.sum(hit) + here - ahead)
    perm[...] = jnp.where(slot == before.astype(jnp.float32), 1.0, 0.0).astype(jnp.bfloat16)

    for parity in range(2):
        for part in range(2):
            for step in range(HALF // LANES):
                at = pl.ds(step * LANES, LANES)
                cos_a = coarse[0, parity, part, :, at]
                sin_a = coarse[1, parity, part, :, at]
                cos_b = fine[0, parity].reshape(NBAND * PAIRS // 8, 8, LANES)
                sin_b = fine[1, parity].reshape(NBAND * PAIRS // 8, 8, LANES)
                value = (cos_a[None] * cos_b - sin_a[None] * sin_b).reshape(NBAND, PAIRS, LANES)
                top = value.astype(jnp.bfloat16)
                table_high[parity, :, pl.ds(part * PAIRS, PAIRS), at] = top
                table_low[parity, :, pl.ds(part * PAIRS, PAIRS), at] = (
                    value - top.astype(jnp.float32)
                ).astype(jnp.bfloat16)

    edge = NT // 16
    tiles = seg // LANES
    number = lax.broadcasted_iota(jnp.int32, (8, LANES), 0) % rows_dev
    begin = jnp.zeros((8, LANES), jnp.int32)
    for r in range(rows_dev):
        begin = jnp.where(number == r, offs[r], begin)
    taper, window = {}, {}
    for tile in (0, 1, tiles - 2, tiles - 1):
        sample = lax.broadcasted_iota(jnp.int32, (8, LANES), 1) + tile * LANES - begin
        inside = (sample >= 0) & (sample < NT)
        near = jnp.minimum(sample, NT - 1 - sample).astype(jnp.float32) + 0.5
        slope = 0.5 * (1.0 - jnp.cos(near * (math.pi / edge)))
        taper[tile] = jnp.where(inside, jnp.where(near < edge, slope, 1.0), 0.0)
        window[tile] = jnp.where(inside, 1.0, 0.0)

    step_chan = 16
    step_rows = step_chan * rows_dev
    half_tiles = HALF // LANES
    fetch.wait()

    def prepare(i, carry):
        at = pl.ds(pl.multiple_of(i * step_chan, step_chan), step_chan)
        x = strain[at].astype(jnp.float32).reshape(step_rows // 8, 8, seg)
        x = [x[:, :, t * LANES : (t + 1) * LANES] for t in range(tiles)]
        total = x[0] * window[0] + x[tiles - 1] * window[tiles - 1]
        for t in range(1, tiles - 1):
            total = total + x[t]
        mean = jnp.sum(total, axis=2, keepdims=True) * (1.0 / NT)
        z = [v - mean for v in x]
        for t in taper:
            z[t] = z[t] * taper[t]
        z[0] = z[0] + z[tiles - 1]
        for t in range(half_tiles):
            fold[0, t] = (z[t] + z[t + half_tiles]).reshape(step_rows, LANES)
            fold[1, t] = (z[t] - z[t + half_tiles]).reshape(step_rows, LANES)
        for parity in range(2):
            for t in range(half_tiles):
                lanes = pl.ds(t * LANES, LANES)
                for r in range(rows_dev):
                    value = fold[parity, t, pl.ds(r, step_chan, stride=rows_dev), :]
                    top = value.astype(jnp.bfloat16)
                    high[r, parity, at, lanes] = top
                    low[r, parity, at, lanes] = (value - top.astype(jnp.float32)).astype(
                        jnp.bfloat16
                    )
        return carry

    lax.fori_loop(0, chan // step_chan, prepare, 0)

    rows = NBAND * SUB
    for r in range(rows_dev):
        for parity in range(2):
            t_high = table_high[parity].reshape(rows, HALF)
            t_low = table_low[parity].reshape(rows, HALF)
            x_high, x_low = high[r, parity], low[r, parity]
            dot = functools.partial(
                lax.dot_general, dimension_numbers=NT_DIMS, preferred_element_type=jnp.float32
            )
            spec[parity] = dot(t_high, x_high) + dot(t_high, x_low) + dot(t_low, x_high)

        off = offs[r]
        pair = lax.broadcasted_iota(jnp.int32, (PAIRS, LANES), 0)
        turn = 2.0 * math.pi / NT
        inner = []
        for parity in range(2):
            angle = (((F_LO + 2 * pair + parity) * off) & (NT - 1)).astype(jnp.float32) * turn
            inner.append((jnp.cos(angle), jnp.sin(angle)))
        band_no = lax.broadcasted_iota(jnp.int32, (NBAND, LANES), 0)
        angle = ((SUB * band_no * off) & (NT - 1)).astype(jnp.float32) * turn
        band_cos, band_sin = jnp.cos(angle), jnp.sin(angle)

        for band in range(NBAND):
            total = None
            for parity in range(2):
                block = spec[parity, pl.ds(band * SUB, SUB), :]
                energy = jnp.sum(block * block, axis=0, keepdims=True)
                total = energy if total is None else total + energy
            scale = lax.rsqrt(total * (1.0 / SUB) + EPSILON)
            bc, bs = band_cos[band : band + 1], band_sin[band : band + 1]
            for parity in range(2):
                ic, is_ = inner[parity]
                cos = ic * bc - is_ * bs
                sin = ic * bs + is_ * bc
                for lane in range(chan // LANES):
                    lanes = pl.ds(lane * LANES, LANES)
                    scale_l = scale[:, lane * LANES : (lane + 1) * LANES]
                    real = spec[parity, pl.ds(band * SUB, PAIRS), lanes] * scale_l
                    imag = spec[parity, pl.ds(band * SUB + PAIRS, PAIRS), lanes] * scale_l
                    for part, value in enumerate((real * cos - imag * sin, real * sin + imag * cos)):
                        start = band * PAIRS * PITCH + (2 * parity + part) * rows_dev + r
                        laid[lane, pl.ds(start, PAIRS, stride=PITCH), :] = value

    per_win = bins_dev * 2 * rows_dev
    pair_rows = 4 * rows_dev
    per_chunk = per_win // CHUNKS
    for w in range(wins):
        white = jnp.concatenate(
            [
                jnp.concatenate(
                    [
                        laid[lane, pl.ds((w * bins_dev // 2 + i) * PITCH, pair_rows), :].astype(
                            jnp.bfloat16
                        )
                        for i in range(bins_dev // 2)
                    ],
                    axis=0,
                )
                for lane in range(chan // LANES)
            ],
            axis=1,
        )
        placed = jnp.dot(white, perm[...], preferred_element_type=jnp.float32).astype(jnp.bfloat16)
        for k in range(CHUNKS):
            pieces[k][w] = placed[k * per_chunk : (k + 1) * per_chunk, :LANES]
        pieces[CHUNKS][w] = placed[:, LANES:]


def front(strain, sources, offsets, mesh_row, wins):
    chan, rows_dev, seg = strain.shape
    rows = NF // wins * 2 * rows_dev
    fine, coarse = table_parts()
    vmem = pl.BlockSpec(memory_space=pltpu.VMEM)
    smem = pl.BlockSpec(memory_space=pltpu.SMEM)
    part = jax.ShapeDtypeStruct((wins, rows // CHUNKS, LANES), jnp.bfloat16)
    return pl.pallas_call(
        functools.partial(front_kernel, rows_dev, wins),
        out_shape=[part] * CHUNKS
        + [
            jax.ShapeDtypeStruct((wins, rows, LANES), jnp.bfloat16),
            jax.ShapeDtypeStruct((chan, chan), jnp.bfloat16),
        ],
        in_specs=[smem, smem, vmem, pl.BlockSpec(memory_space=pl.ANY), vmem, vmem],
        out_specs=[vmem] * (CHUNKS + 2),
        scratch_shapes=[
            pltpu.VMEM(strain.shape, strain.dtype),
            pltpu.VMEM((rows_dev, 2, chan, HALF), jnp.bfloat16),
            pltpu.VMEM((rows_dev, 2, chan, HALF), jnp.bfloat16),
            pltpu.VMEM((2, NBAND, SUB, HALF), jnp.bfloat16),
            pltpu.VMEM((2, NBAND, SUB, HALF), jnp.bfloat16),
            pltpu.VMEM((2, NBAND * SUB, chan), jnp.float32),
            pltpu.VMEM((chan // LANES, NBAND * PAIRS * PITCH, LANES), jnp.float32),
            pltpu.VMEM((2, HALF // LANES, 16 * rows_dev, LANES), jnp.float32),
            pltpu.SemaphoreType.DMA,
        ],
        compiler_params=pltpu.CompilerParams(vmem_limit_bytes=56 * 2**20),
        name="front",
    )(offsets, mesh_row, sources, strain, jnp.asarray(fine), jnp.asarray(coarse))


def cross_kernel(rows_dev, wins, records, *refs):
    owners_refs, (other, perm, select), out, laid = refs[:-5], refs[-5:-2], refs[-2], refs[-1]
    mine = owners_refs[0]
    columns = select.shape[1] // LANES
    owners_refs = owners_refs[-columns:]
    depth = 2 * rows_dev * wins
    group = 256 // depth
    near = 2 * rows_dev * group
    width = wins * near
    sources = select.shape[0]
    scale = 1.0 / records

    lane = lax.broadcasted_iota(jnp.int32, (1, width), 1)
    row_no = lax.broadcasted_iota(jnp.int32, (width, width), 0)
    col_no = lax.broadcasted_iota(jnp.int32, (width, width), 1)
    first = (col_no // rows_dev) % 2 == 0
    turn = jnp.where(
        first & (row_no == col_no + rows_dev),
        1.0,
        jnp.where(jnp.logical_not(first) & (row_no == col_no - rows_dev), -1.0, 0.0),
    ).astype(jnp.bfloat16)
    keep = [((lane // (2 * rows_dev)) % group == b).astype(jnp.bfloat16) for b in range(group)]

    for g in range(JBLOCK // group):
        at = pl.ds(g * near, near)

        def rows_of(ref):
            return ref[:, at, :].reshape(width, LANES)

        slots = jnp.concatenate((rows_of(mine), rows_of(other)), axis=1)
        receivers = lax.dot_general(
            slots, perm[...], NT_DIMS, preferred_element_type=jnp.float32
        ).astype(jnp.bfloat16)
        held = jnp.concatenate([rows_of(ref) for ref in owners_refs], axis=1)
        picked = lax.dot_general(
            select[...], held, NT_DIMS, preferred_element_type=jnp.float32
        ).astype(jnp.bfloat16)
        turned = jnp.dot(picked, turn, preferred_element_type=jnp.float32).astype(jnp.bfloat16)
        for b in range(group):
            both = jnp.concatenate((picked * keep[b], turned * keep[b]), axis=0)
            product = jnp.dot(both, receivers, preferred_element_type=jnp.float32)
            for part in range(2):
                for half in range(product.shape[1] // LANES):
                    laid[part, half, pl.ds(g * group + b, sources, stride=PITCH), :] = product[
                        part * sources : (part + 1) * sources, half * LANES : (half + 1) * LANES
                    ]

    few = 32

    def emit(i, carry):
        for n in range(few):
            rows = pl.ds((i * few + n) * PITCH, JBLOCK)
            for part in range(2):
                for half in range(laid.shape[1]):
                    value = (laid[part, half, rows, :] * scale).astype(jnp.bfloat16)
                    out[part, i * few + n, :, half * LANES : (half + 1) * LANES] = value
        return carry

    lax.fori_loop(0, sources // few, emit, 0)


def cross(k, whole, owners, other, perm, select, shape, records, rows_dev):
    wins, rows, _ = owners[0].shape
    sources, chan = shape[1], shape[3]
    per_block = JBLOCK * 2 * rows_dev
    steps = rows // per_block
    piece = pl.BlockSpec((wins, per_block, LANES), lambda g: (0, g, 0))
    later = pl.BlockSpec((wins, per_block, LANES), lambda g: (0, k * steps + g, 0))
    fixed = lambda array: pl.BlockSpec(array.shape, lambda g: (0, 0))
    args = list(owners) + [other, perm, select]
    specs = [piece] * len(owners) + [later, fixed(perm), fixed(select)]
    body = functools.partial(cross_kernel, rows_dev, wins, records)
    aliases = {}
    if whole is not None:
        inner, count = body, len(args)
        body = lambda *refs: inner(*refs[:count], *refs[count + 1 :])
        aliases = {count: 0}
        args.append(whole)
        specs.append(pl.BlockSpec(memory_space=pl.ANY))
    return pl.pallas_call(
        body,
        grid=(steps,),
        out_shape=jax.ShapeDtypeStruct(shape, jnp.bfloat16),
        in_specs=specs,
        out_specs=pl.BlockSpec((2, sources, JBLOCK, chan), lambda g: (0, 0, k * steps + g, 0)),
        scratch_shapes=[pltpu.VMEM((2, chan // LANES, sources * PITCH, LANES), jnp.float32)],
        input_output_aliases=aliases,
        compiler_params=pltpu.CompilerParams(vmem_limit_bytes=56 * 2**20),
        name=f"cross{k}",
    )(*args)


def body(recs, wins, strain, sources, offsets):
    chan, rows_dev, _ = strain.shape
    me = lax.axis_index("rec")
    owner = sources // chan
    rank = jnp.sum(
        (owner[None, :] == owner[:, None]) & (sources[None, :] < sources[:, None]), axis=1
    ).astype(jnp.int32)
    if recs == 4:
        order = me ^ jnp.arange(4, dtype=jnp.int32)
    else:
        order = jnp.arange(recs, dtype=jnp.int32)
    place = jnp.arange(LANES, dtype=jnp.int32)
    select = (
        (owner[:, None, None] == order[None, :, None]) & (rank[:, None, None] == place[None, None, :])
    ).astype(jnp.bfloat16).reshape(sources.shape[0], recs * LANES)

    *pieces, perm = front(strain, sources[None], offsets, me.astype(jnp.int32)[None], wins)

    def swap(array, bit):
        return lax.ppermute(array, "rec", [(i, i ^ bit) for i in range(recs)])

    def spread(array):
        return lax.all_to_all(array, "win", split_axis=0, concat_axis=0, tiled=True)

    owners = []
    for k in range(CHUNKS):
        mine = spread(pieces[k])
        if recs == 4:
            along_x, along_y = swap(mine, 1), swap(mine, 2)
            far = swap(along_x, 2) if k % 2 == 0 else swap(along_y, 1)
            owners.append((mine, along_x, along_y, far))
        else:
            gathered = lax.all_gather(mine, "rec", axis=0)
            owners.append((mine,) + tuple(gathered[i] for i in range(recs)))
    other = spread(pieces[CHUNKS])
    shape = (2, sources.shape[0], NF // wins, chan)
    whole = None
    for k in range(CHUNKS):
        whole = cross(k, whole, owners[k], other, perm, select, shape, rows_dev * wins, rows_dev)
    return whole


def solution(mesh):
    recs, wins = mesh.shape["rec"], mesh.shape["win"]
    placed = (P("rec", "win", None), P(), P("win"))
    return jax.shard_map(
        functools.partial(body, recs, wins),
        mesh=mesh,
        in_specs=placed,
        out_specs=P(None, None, "win", "rec"),
        check_vma=False,
    )
```
